32 devices in a mesh: rep: 4 (over x, core), fsdp: 2 (over y), seq: 4 (over z).
Axes of the slice: x: 2, y: 2, z: 4, core: 2. Of those that a mesh axis runs over, the one named last changes fastest.
Arguments:
- tokens: bfloat16 [8, 512, 1024], P(('rep', 'fsdp'), 'seq'), may hold values from -6 to 6
- conditioning: bfloat16 [8, 1024], P(('rep', 'fsdp')), may hold values from -6 to 6
- cotangent: bfloat16 [8, 512, 1024], P(('rep', 'fsdp'), 'seq'), may hold values from -6 to 6
- ada_weight: bfloat16 [1024, 6144], P('fsdp'), may hold values from -0.1875 to 0.1875
- ada_bias: bfloat16 [6144], P('fsdp'), may hold values from -3 to 3
- qkv_weight: bfloat16 [1024, 3072], P('fsdp'), may hold values from -0.1875 to 0.1875
- qv_bias: bfloat16 [2048], P('fsdp'), may hold values from -3 to 3
- proj_weight: bfloat16 [1024, 1024], P('fsdp'), may hold values from -1 to 1
- proj_bias: bfloat16 [1024], P('fsdp'), may hold values from -3 to 3
- fc1_weight: bfloat16 [1024, 4096], P('fsdp'), may hold values from -0.1875 to 0.1875
- fc1_bias: bfloat16 [4096], P('fsdp'), may hold values from -3 to 3
- fc2_weight: bfloat16 [4096, 1024], P('fsdp'), may hold values from -0.09375 to 0.09375
- fc2_bias: bfloat16 [1024], P('fsdp'), may hold values from -3 to 3
Outputs:
- output: bfloat16 [8, 512, 1024], P(('rep', 'fsdp'), 'seq')
- tokens_grad: float32 [8, 512, 1024], P(('rep', 'fsdp'), 'seq')
- cond_grad: float32 [8, 1024], P(('rep', 'fsdp'))
- ada_weight_grad: float32 [1024, 6144], P('fsdp')
- ada_bias_grad: float32 [6144], P('fsdp')
- qkv_weight_grad: float32 [1024, 3072], P('fsdp')
- qv_bias_grad: float32 [2048], P('fsdp')
- proj_weight_grad: float32 [1024, 1024], P('fsdp')
- proj_bias_grad: float32 [1024], P('fsdp')
- fc1_weight_grad: float32 [1024, 4096], P('fsdp')
- fc1_bias_grad: float32 [4096], P('fsdp')
- fc2_weight_grad: float32 [4096, 1024], P('fsdp')
- fc2_bias_grad: float32 [1024], P('fsdp')
The draws below stay inside these ranges and needn't reach their ends.
All inputs are finite; a program needn't handle non-finite values.
Results may differ from the reference program's by a relative error of at most 0.012.
The reference program's roundings to bfloat16 on the way count: a program that leaves them out, or rounds other values in their place, can miss the bound.
Values may be sent and summed in bfloat16 or wider, within the bound.
No kernel may reach another device: no remote copies, remote signals or barrier semaphores. Data moves between devices by JAX's collectives and lax.ppermute only.
A program may use at most 256 MiB of HBM per device.

```python
import jax
import jax.numpy as jnp
from jax import lax

D = 1024
HEADS = 16
HEAD_DIM = 64
FF = 4096
C = 1024
SEQLEN = 512
LATENTS = 8


def levels(own_key, shape, shards, low, largest):
    level, own = 1.0, jax.random.fold_in(own_key, 6)
    for axis_at, blocks in shards:
        steps = jnp.exp(jax.random.uniform(jax.random.fold_in(own, axis_at), (blocks,), jnp.float32, low / len(shards), largest / len(shards)))
        level = level * jnp.repeat(steps, shape[axis_at] // blocks).reshape([-1 if axis == axis_at else 1 for axis in range(len(shape))])
    return level


def noise(own_key, extent, scale, bound, pieces=(), dtype=jnp.bfloat16):
    drawn = scale * jax.random.normal(own_key, extent, jnp.float32)
    if pieces:
        drawn = drawn * levels(own_key, extent, pieces, -0.22, 0.18)
    return jnp.clip(drawn, -bound, bound).astype(dtype)


def setup_inputs(seed: int = 0) -> dict:
    streams_of = jax.random.split(jax.random.key(seed), 14)
    tokens = noise(streams_of[0], (LATENTS, SEQLEN, D), 1.0, 6.0, ((0, 8), (1, 4)))
    conditioning = noise(streams_of[1], (LATENTS, C), 1.0, 6.0, ((0, 8),))
    cotangent = noise(streams_of[2], (LATENTS, SEQLEN, D), 1.0, 6.0, ((0, 8), (1, 4)))
    ada_weight = noise(streams_of[3], (C, 6 * D), C ** -0.5, 0.1875, ((0, 2),))
    ada_bias = noise(streams_of[4], (6 * D,), 0.5, 3.0, ((0, 2),))
    qkv_weight = noise(streams_of[5], (D, 3 * D), D ** -0.5, 0.1875, ((0, 2),))
    qv_bias = noise(streams_of[6], (2 * D,), 0.5, 3.0, ((0, 2),))
    proj_weight = noise(streams_of[7], (D, D), (D * 16 // SEQLEN) ** -0.5, 1.0, ((0, 2),))
    proj_bias = noise(streams_of[8], (D,), 0.5, 3.0, ((0, 2),))
    fc1_weight = noise(streams_of[9], (D, FF), D ** -0.5, 0.1875, ((0, 2),))
    fc1_bias = noise(streams_of[10], (FF,), 0.5, 3.0, ((0, 2),))
    fc2_weight = noise(streams_of[11], (FF, D), FF ** -0.5, 0.09375, ((0, 2),))
    fc2_bias = noise(streams_of[12], (D,), 0.5, 3.0, ((0, 2),))
    return {"tokens": tokens, "conditioning": conditioning, "cotangent": cotangent, "ada_weight": ada_weight, "ada_bias": ada_bias, "qkv_weight": qkv_weight, "qv_bias": qv_bias, "proj_weight": proj_weight, "proj_bias": proj_bias, "fc1_weight": fc1_weight, "fc1_bias": fc1_bias, "fc2_weight": fc2_weight, "fc2_bias": fc2_bias}


EPSILON = 1e-06
TANH_ROOT = 0.7978845608028654
CUBIC_COEF = 0.044715

def product(left_op, right_op):
    return jnp.dot(left_op, right_op, preferred_element_type=jnp.float32)

def product_tn(left_op, right_op):
    return lax.dot_general(left_op, right_op, (((0,), (0,)), ((), ())), preferred_element_type=jnp.float32)

def product_nt(left_op, right_op):
    return lax.dot_general(left_op, right_op, (((1,), (1,)), ((), ())), preferred_element_type=jnp.float32)

def rounded(values):
    return lax.optimization_barrier(values.astype(jnp.bfloat16)).astype(jnp.float32)

def gelu_parts(pre_act):
    tanh_val = jnp.tanh(TANH_ROOT * (pre_act + CUBIC_COEF * pre_act * pre_act * pre_act))
    gelu_val = 0.5 * pre_act * (1.0 + tanh_val)
    gelu_slope = 0.5 * (1.0 + tanh_val) + 0.5 * pre_act * (1.0 - tanh_val * tanh_val) * TANH_ROOT * (1.0 + 3.0 * CUBIC_COEF * pre_act * pre_act)
    return (gelu_val, gelu_slope)

def layer_norm(values):
    center = values - lax.optimization_barrier(jnp.mean(values, axis=-1, keepdims=True))
    inv_std = lax.rsqrt(lax.optimization_barrier(jnp.mean(center * center, axis=-1, keepdims=True)) + EPSILON)
    return (center * inv_std, inv_std)

def norm_back(normed, inv_std, grad_in):
    return inv_std * (grad_in - lax.optimization_barrier(jnp.mean(grad_in, axis=-1, keepdims=True)) - normed * lax.optimization_barrier(jnp.mean(grad_in * normed, axis=-1, keepdims=True)))

def silu_slope(condition):
    sigmoid_c = jax.nn.sigmoid(condition)
    return sigmoid_c * (1.0 + condition * (1.0 - sigmoid_c))

def split_heads(values):
    return values.astype(jnp.float32).reshape(values.shape[0], HEADS, values.shape[1] // HEADS)

def attend(query_rows, key_rows, value_rows):
    score_scale = HEAD_DIM ** (-0.5)
    query_heads, key_heads, value_heads = (split_heads(query_rows), split_heads(key_rows), split_heads(value_rows))
    scores = jnp.einsum('qhd,khd->hqk', query_heads, key_heads) * score_scale
    row_max = lax.optimization_barrier(jnp.max(scores, axis=-1, keepdims=True))
    exponent = jnp.exp(scores - row_max)
    row_total = lax.optimization_barrier(jnp.sum(exponent, axis=-1, keepdims=True))
    attn_probs = rounded(exponent / row_total)
    attended = jnp.einsum('hqk,khd->qhd', attn_probs, value_heads)
    attended = attended.reshape(query_rows.shape[0], query_rows.shape[1]).astype(jnp.bfloat16)
    return (attended, row_max + jnp.log(row_total))

def attend_back(query_rows, key_rows, value_rows, log_total, attended_grad):
    score_scale = HEAD_DIM ** (-0.5)
    query_heads, key_heads, value_heads = (split_heads(query_rows), split_heads(key_rows), split_heads(value_rows))
    grad_heads = split_heads(attended_grad)
    scores = jnp.einsum('qhd,khd->hqk', query_heads, key_heads) * score_scale
    probs_again = jnp.exp(scores - log_total)
    value_grad = jnp.einsum('hqk,qhd->khd', rounded(probs_again), grad_heads)
    prob_grad = jnp.einsum('qhd,khd->hqk', grad_heads, value_heads)
    row_delta = lax.optimization_barrier(jnp.sum(probs_again * prob_grad, axis=-1, keepdims=True))
    score_grad = rounded(probs_again * (prob_grad - row_delta) * score_scale)
    query_grad = jnp.einsum('hqk,khd->qhd', score_grad, key_heads)
    key_grad = jnp.einsum('hqk,qhd->khd', score_grad, query_heads)
    model_width = query_rows.shape[1]
    return (query_grad.reshape(query_rows.shape[0], model_width), key_grad.reshape(key_rows.shape[0], model_width), value_grad.reshape(key_rows.shape[0], model_width))

def latent_pass(latent_tokens, condition_row, latent_cot, weights):
    ada_weight, ada_bias, qkv_weight, qv_bias, proj_weight, proj_bias, fc1_weight, fc1_bias, fc2_weight, fc2_bias = weights
    model_width = latent_tokens.shape[1]
    cond_f = condition_row.astype(jnp.float32)
    silu_cond = jax.nn.silu(cond_f).astype(jnp.bfloat16)
    mods = product(silu_cond, ada_weight)[0] + ada_bias.astype(jnp.float32)
    shift_attn, scale_attn, gate_attn, shift_mlp, scale_mlp, gate_mlp = jnp.split(mods, 6)
    tokens_f = latent_tokens.astype(jnp.float32)
    normed1, inv_std1 = layer_norm(tokens_f)
    hidden1 = (normed1 * (1.0 + scale_attn) + shift_attn).astype(jnp.bfloat16)
    qkv_rows = product(hidden1, qkv_weight)
    qv_float = qv_bias.astype(jnp.float32)
    query_rows = (qkv_rows[:, :model_width] + qv_float[:model_width]).astype(jnp.bfloat16)
    key_rows = qkv_rows[:, model_width:2 * model_width].astype(jnp.bfloat16)
    value_rows = (qkv_rows[:, 2 * model_width:] + qv_float[model_width:]).astype(jnp.bfloat16)
    attended, log_total = attend(query_rows, key_rows, value_rows)
    branch = product(attended, proj_weight) + proj_bias.astype(jnp.float32)
    middle = tokens_f + gate_attn * branch
    normed2, inv_std2 = layer_norm(middle)
    hidden2 = (normed2 * (1.0 + scale_mlp) + shift_mlp).astype(jnp.bfloat16)
    pre_act = product(hidden2, fc1_weight) + fc1_bias.astype(jnp.float32)
    gelu_val, gelu_slope = gelu_parts(pre_act)
    active = gelu_val.astype(jnp.bfloat16)
    mlp_out = product(active, fc2_weight) + fc2_bias.astype(jnp.float32)
    output = (middle + gate_mlp * mlp_out).astype(jnp.bfloat16)
    cot_f = latent_cot.astype(jnp.float32)
    mlp_grad = (gate_mlp * cot_f).astype(jnp.bfloat16)
    gate_mlp_grad = lax.optimization_barrier(jnp.sum(cot_f * mlp_out, axis=0))
    fc2_weight_grad = product_tn(active, mlp_grad)
    fc2_bias_grad = lax.optimization_barrier(jnp.sum(mlp_grad.astype(jnp.float32), axis=0))
    pre_grad = (product_nt(mlp_grad, fc2_weight) * gelu_slope).astype(jnp.bfloat16)
    fc1_weight_grad = product_tn(hidden2, pre_grad)
    fc1_bias_grad = lax.optimization_barrier(jnp.sum(pre_grad.astype(jnp.float32), axis=0))
    hidden2_grad = product_nt(pre_grad, fc1_weight)
    shift_mlp_grad = lax.optimization_barrier(jnp.sum(hidden2_grad, axis=0))
    scale_mlp_grad = lax.optimization_barrier(jnp.sum(hidden2_grad * normed2, axis=0))
    middle_grad = cot_f + norm_back(normed2, inv_std2, hidden2_grad * (1.0 + scale_mlp))
    gate_attn_grad = lax.optimization_barrier(jnp.sum(middle_grad * branch, axis=0))
    branch_grad = (gate_attn * middle_grad).astype(jnp.bfloat16)
    proj_weight_grad = product_tn(attended, branch_grad)
    proj_bias_grad = lax.optimization_barrier(jnp.sum(branch_grad.astype(jnp.float32), axis=0))
    attended_grad = product_nt(branch_grad, proj_weight).astype(jnp.bfloat16)
    query_grad, key_grad, value_grad = attend_back(query_rows, key_rows, value_rows, log_total, attended_grad)
    qkv_grad = jnp.concatenate([query_grad.astype(jnp.bfloat16), key_grad.astype(jnp.bfloat16), value_grad.astype(jnp.bfloat16)], axis=1)
    qkv_weight_grad = product_tn(hidden1, qkv_grad)
    qv_bias_grad = jnp.concatenate([lax.optimization_barrier(jnp.sum(qkv_grad[:, :model_width].astype(jnp.float32), axis=0)), lax.optimization_barrier(jnp.sum(qkv_grad[:, 2 * model_width:].astype(jnp.float32), axis=0))])
    hidden1_grad = product_nt(qkv_grad, qkv_weight)
    shift_attn_grad = lax.optimization_barrier(jnp.sum(hidden1_grad, axis=0))
    scale_attn_grad = lax.optimization_barrier(jnp.sum(hidden1_grad * normed1, axis=0))
    tokens_grad = middle_grad + norm_back(normed1, inv_std1, hidden1_grad * (1.0 + scale_attn))
    mods_grad = jnp.concatenate([shift_attn_grad, scale_attn_grad, gate_attn_grad, shift_mlp_grad, scale_mlp_grad, gate_mlp_grad])
    ada_weight_grad = lax.dot_general(silu_cond.astype(jnp.float32), mods_grad[None, :], (((0,), (0,)), ((), ())), precision=lax.Precision.HIGHEST)
    cond_grad = lax.dot_general(mods_grad[None, :], ada_weight.astype(jnp.float32), (((1,), (1,)), ((), ())), precision=lax.Precision.HIGHEST) * silu_slope(cond_f)
    grads = (ada_weight_grad, mods_grad, qkv_weight_grad, qv_bias_grad, proj_weight_grad, proj_bias_grad, fc1_weight_grad, fc1_bias_grad, fc2_weight_grad, fc2_bias_grad)
    return (output, tokens_grad, cond_grad[0], grads)

def reference(tokens, conditioning, cotangent, ada_weight, ada_bias, qkv_weight, qv_bias, proj_weight, proj_bias, fc1_weight, fc1_bias, fc2_weight, fc2_bias):
    weights = (ada_weight, ada_bias, qkv_weight, qv_bias, proj_weight, proj_bias, fc1_weight, fc1_bias, fc2_weight, fc2_bias)

    def scan_step(totals, latent_items):
        latent_tokens, condition, latent_cot = latent_items
        output, tokens_grad, cond_grad, grads = latent_pass(latent_tokens, condition[None, :], latent_cot, weights)
        summed = tuple((total_item + grad_item for total_item, grad_item in zip(totals, grads)))
        return (summed, (output, tokens_grad, cond_grad))
    zero_grads = tuple((jnp.zeros(weight_item.shape, jnp.float32) for weight_item in weights))
    totals, stacked = lax.scan(scan_step, zero_grads, (tokens, conditioning, cotangent))
    return (stacked[0], stacked[1], stacked[2], totals[0], totals[1], totals[2], totals[3], totals[4], totals[5], totals[6], totals[7], totals[8], totals[9])
```

```python
import functools

import jax
import jax.numpy as jnp
from jax import lax
from jax.experimental import pallas as pl
from jax.experimental.pallas import tpu as pltpu
from jax.sharding import PartitionSpec as P

HEADS = 16
HEAD_DIM = 64


EPSILON = 1e-06
TANH_ROOT = 0.7978845608028654
CUBIC_COEF = 0.044715

F32 = jnp.float32
BF16 = jnp.bfloat16


def product(left_op, right_op):
    return jnp.dot(left_op, right_op, preferred_element_type=F32)


def product_tn(left_op, right_op):
    return lax.dot_general(
        left_op, right_op, (((0,), (0,)), ((), ())), preferred_element_type=F32
    )


def product_nt(left_op, right_op):
    return lax.dot_general(
        left_op, right_op, (((1,), (1,)), ((), ())), preferred_element_type=F32
    )


def gelu_parts(pre_act):
    tanh_val = jnp.tanh(TANH_ROOT * (pre_act + CUBIC_COEF * pre_act * pre_act * pre_act))
    gelu_val = 0.5 * pre_act * (1.0 + tanh_val)
    gelu_slope = 0.5 * (1.0 + tanh_val) + 0.5 * pre_act * (
        1.0 - tanh_val * tanh_val
    ) * TANH_ROOT * (1.0 + 3.0 * CUBIC_COEF * pre_act * pre_act)
    return (gelu_val, gelu_slope)


def layer_norm(values):
    center = values - jnp.mean(values, axis=-1, keepdims=True)
    inv_std = lax.rsqrt(jnp.mean(center * center, axis=-1, keepdims=True) + EPSILON)
    return (center * inv_std, inv_std)


def norm_back(normed, inv_std, grad_in):
    return inv_std * (
        grad_in
        - jnp.mean(grad_in, axis=-1, keepdims=True)
        - normed * jnp.mean(grad_in * normed, axis=-1, keepdims=True)
    )


def silu_slope(condition):
    sigmoid_c = jax.nn.sigmoid(condition)
    return sigmoid_c * (1.0 + condition * (1.0 - sigmoid_c))


def swap(value, axis, mask):
    size = lax.axis_size(axis)
    return lax.ppermute(value, axis, [(i, i ^ mask) for i in range(size)])


def masks(axis):
    size, found, mask = lax.axis_size(axis), [], 1
    while mask < size:
        found.append(mask)
        mask *= 2
    return found


def gather_rows(value, steps):
    for axis, mask in steps:
        value = jnp.concatenate([value, swap(value, axis, mask)], axis=0)
    return value


def natural(stack, axis):
    me = lax.axis_index(axis)
    return jnp.concatenate(
        [lax.dynamic_slice_in_dim(stack, me ^ i, 1, 0) for i in range(stack.shape[0])], axis=0
    )


def whole_weight(weight, relay):
    groups = lax.axis_size("fsdp")
    if groups != 2:
        return [(jnp.int32(0), lax.all_gather(weight, "fsdp", axis=0, tiled=True))]
    rows = weight.shape[0]
    me = lax.axis_index("fsdp")
    axis, mask = relay
    far = jnp.where(lax.axis_index(axis) & mask, 2, 0)
    here = far + (lax.axis_index("rep") & 1)
    piece = rows // 4
    first = swap(lax.dynamic_slice_in_dim(weight, here * piece, piece, 0), "fsdp", 1)
    second = swap(first, axis, mask)
    third = swap(first, "rep", 1)
    fourth = swap(second, "rep", 1)
    peer = (1 - me) * rows
    return [
        (me * rows, weight),
        (peer + here * piece, first),
        (peer + (here ^ 1) * piece, third),
        (peer + (here ^ 2) * piece, second),
        (peer + (here ^ 3) * piece, fourth),
    ]


ANY = pl.BlockSpec(memory_space=pl.ANY)


def full(shape):
    return pl.BlockSpec(shape, lambda *_: (0,) * len(shape))


def cost(flops, nbytes, trans=0):
    return pl.CostEstimate(flops=int(flops), bytes_accessed=int(nbytes), transcendentals=int(trans))


def columns_kernel(sizes, tile, back, finish, n_extra, n_out, offs, act, *refs):
    n = len(sizes)
    weights, extras, outs = refs[:n], refs[n : n + n_extra], refs[n + n_extra : n + n_extra + n_out]
    buf, sems = refs[n + n_extra + n_out : n + n_extra + n_out + 2]
    step, steps = pl.program_id(0), pl.num_programs(0)
    slot = lax.rem(step, 2)

    def copies(at, into):
        cols = pl.ds(pl.multiple_of(at * tile, tile), tile)
        return [
            pltpu.make_async_copy(
                w.at[:, cols],
                buf.at[into, pl.ds(pl.multiple_of(offs[b], 16), sizes[b]), :],
                sems.at[into, b],
            )
            for b, w in enumerate(weights)
        ]

    @pl.when(step == 0)
    def _():
        for c in copies(0, 0):
            c.start()

    @pl.when(step + 1 < steps)
    def _():
        for c in copies(step + 1, 1 - slot):
            c.start()

    for c in copies(step, slot):
        c.wait()
    if back:
        acc = refs[-1]

        @pl.when(step == 0)
        def _():
            acc[...] = jnp.zeros_like(acc)

        acc[...] += product_nt(act[...].reshape(act.shape[-2:]), buf[slot])

        @pl.when(step == steps - 1)
        def _():
            finish(acc[...], extras, outs)
    else:
        finish(product(act[...], buf[slot]), extras, outs)


def columns_call(name, act, act_spec, blocks, tile, back, finish, extras, extra_specs, outs, out_specs):
    offs = jnp.stack([o for o, _ in blocks]).astype(jnp.int32)
    weights = [w for _, w in blocks]
    sizes = [w.shape[0] for w in weights]
    depth, width = sum(sizes), weights[0].shape[1]
    n_tok = act.shape[-2]
    scratch = [pltpu.VMEM((2, depth, tile), BF16), pltpu.SemaphoreType.DMA((2, len(sizes)))]
    if back:
        scratch.append(pltpu.VMEM((n_tok, depth), F32))
    return pl.pallas_call(
        functools.partial(columns_kernel, sizes, tile, back, finish, len(extras), len(outs)),
        grid_spec=pltpu.PrefetchScalarGridSpec(
            num_scalar_prefetch=1,
            grid=(width // tile,),
            in_specs=[act_spec] + [ANY] * len(weights) + list(extra_specs),
            out_specs=list(out_specs),
            scratch_shapes=scratch,
        ),
        out_shape=list(outs),
        compiler_params=pltpu.CompilerParams(dimension_semantics=("arbitrary",)),
        cost_estimate=cost(2 * n_tok * depth * width, 2 * depth * width),
        name=name,
    )(offs, act, *weights, *extras)


def mlp_kernel(plan, tile, offs, active, slope, mlp_grad, bias, *refs):
    n = 1 + max(b for b, _ in plan)
    weights = refs[:n]
    out, pre_grad, buf, sems = refs[n:]

    def copy(s):
        b, at = plan[s]
        return pltpu.make_async_copy(
            weights[b].at[pl.ds(at, tile), :], buf.at[s % 2], sems.at[s % 2]
        )

    copy(0).start()
    out[...] = jnp.broadcast_to(bias[...], out.shape)
    for s in range(len(plan)):
        if s + 1 < len(plan):
            copy(s + 1).start()
        copy(s).wait()
        cols = pl.ds(pl.multiple_of(offs[s], 128), tile)
        out[...] += product(active[:, cols], buf[s % 2])
        pre_grad[:, cols] = (product_nt(mlp_grad[...], buf[s % 2]) * slope[:, cols]).astype(BF16)


def mlp_call(active, slope, mlp_grad, bias, blocks):
    n_tok, hidden = active.shape
    width = mlp_grad.shape[1]
    tile = min([w.shape[0] for _, w in blocks] + [512])
    plan, offs = [], []
    for b, (o, w) in enumerate(blocks):
        for at in range(0, w.shape[0], tile):
            plan.append((b, at))
            offs.append(o + at)
    vm = pl.BlockSpec(memory_space=pltpu.VMEM)
    return pl.pallas_call(
        functools.partial(mlp_kernel, plan, tile),
        in_specs=[pl.BlockSpec(memory_space=pltpu.SMEM)] + [vm] * 4 + [ANY] * len(blocks),
        out_specs=[vm, vm],
        out_shape=[
            jax.ShapeDtypeStruct((n_tok, width), F32),
            jax.ShapeDtypeStruct((n_tok, hidden), BF16),
        ],
        scratch_shapes=[pltpu.VMEM((2, tile, width), BF16), pltpu.SemaphoreType.DMA((2,))],
        cost_estimate=cost(4 * n_tok * hidden * width, 2 * hidden * width),
        name="mlp_both",
    )(jnp.stack(offs).astype(jnp.int32), active, slope, mlp_grad, bias, *[w for _, w in blocks])


def softmax_of(query, key):
    scores = product_nt(query, key) * (HEAD_DIM**-0.5)
    exponent = jnp.exp(scores - jnp.max(scores, axis=-1, keepdims=True))
    return exponent * (1.0 / jnp.sum(exponent, axis=-1, keepdims=True))


def attend_kernel(n, width, *refs):
    blocks, out = refs[:n], refs[n]
    n_tok = blocks[0].shape[0]

    def part(at):
        return jnp.concatenate([b[:, at : at + HEAD_DIM] for b in blocks], axis=0)

    for head in range(0, width, HEAD_DIM):
        probs = softmax_of(part(head), part(width + head)).astype(BF16)
        attended = product(probs, part(2 * width + head)).astype(BF16)
        for j in range(n):
            out[j, :, head : head + HEAD_DIM] = attended[j * n_tok : (j + 1) * n_tok]


def attend_call(blocks):
    n, n_tok, width = len(blocks), blocks[0].shape[0], blocks[0].shape[1] // 3
    vm = pl.BlockSpec(memory_space=pltpu.VMEM)
    pairs = (n * n_tok) ** 2
    return pl.pallas_call(
        functools.partial(attend_kernel, n, width),
        in_specs=[vm] * n,
        out_specs=vm,
        out_shape=jax.ShapeDtypeStruct((n, n_tok, width), BF16),
        cost_estimate=cost(4 * pairs * width, 8 * n * n_tok * width, pairs * width // HEAD_DIM),
        name="attend",
    )(*blocks)


def attend_back_kernel(n, width, *refs):
    blocks, grads, out = refs[:n], refs[n : 2 * n], refs[2 * n]
    n_tok = blocks[0].shape[0]

    def part(of, at):
        return jnp.concatenate([b[:, at : at + HEAD_DIM] for b in of], axis=0)

    scale = HEAD_DIM**-0.5
    for head in range(0, width, HEAD_DIM):
        query, key = part(blocks, head), part(blocks, width + head)
        value, grad = part(blocks, 2 * width + head), part(grads, head)
        probs = softmax_of(query, key)
        prob_grad = product_nt(grad, value)
        row_delta = jnp.sum(probs * prob_grad, axis=-1, keepdims=True)
        score_grad = (probs * (prob_grad - row_delta) * scale).astype(BF16)
        parts = (
            product(score_grad, key),
            product_tn(score_grad, query),
            product_tn(probs.astype(BF16), grad),
        )
        for at, value_of in enumerate(parts):
            rounded = value_of.astype(BF16)
            for j in range(n):
                out[j, :, at * width + head : at * width + head + HEAD_DIM] = rounded[
                    j * n_tok : (j + 1) * n_tok
                ]


def attend_back_call(blocks, grads):
    n, n_tok, width = len(blocks), blocks[0].shape[0], blocks[0].shape[1] // 3
    vm = pl.BlockSpec(memory_space=pltpu.VMEM)
    pairs = (n * n_tok) ** 2
    return pl.pallas_call(
        functools.partial(attend_back_kernel, n, width),
        in_specs=[vm] * (2 * n),
        out_specs=vm,
        out_shape=jax.ShapeDtypeStruct((n, n_tok, 3 * width), BF16),
        cost_estimate=cost(10 * pairs * width, 14 * n * n_tok * width, pairs * width // HEAD_DIM),
        name="attend_back",
    )(*blocks, *grads)


def heads_kernel(n, parts, me, *refs):
    blocks, out = refs[:n], refs[n]
    width = blocks[0].shape[1] // parts
    for j in range(n):
        for p in range(parts):
            at = pl.multiple_of(p * n * width + (me[0] ^ j) * width, 128)
            out[:, pl.ds(at, width)] = blocks[j][:, p * width : (p + 1) * width]


def heads_call(blocks, parts):
    n, (n_tok, width) = len(blocks), blocks[0].shape
    vm = pl.BlockSpec(memory_space=pltpu.VMEM)
    return pl.pallas_call(
        functools.partial(heads_kernel, n, parts),
        in_specs=[pl.BlockSpec(memory_space=pltpu.SMEM)] + [vm] * n,
        out_specs=vm,
        out_shape=jax.ShapeDtypeStruct((n_tok, n * width), BF16),
        cost_estimate=cost(0, 4 * n * n_tok * width),
        name="heads",
    )(lax.axis_index("seq").reshape(1).astype(jnp.int32), *blocks)


def grad_kernel(n, at, spot, *refs):
    acts, grads, out, flipped = refs[:n], refs[n : 2 * n], refs[2 * n], refs[2 * n + 1]

    @pl.when(pl.program_id(0) == 0)
    def _():
        row = 0
        for a in acts:
            flipped[:, row : row + a.shape[0]] = a[...].T
            row += a.shape[0]

    rows = jnp.concatenate([g[...] for g in grads], axis=0)
    out[0] = product(flipped[...], rows).astype(BF16)


def grad_call(acts, grads, spot, count, first, blocks):
    depth, width = acts[0].shape[1], grads[0].shape[1] // blocks
    tokens = sum(a.shape[0] for a in acts)
    return pl.pallas_call(
        functools.partial(grad_kernel, len(acts), first),
        grid_spec=pltpu.PrefetchScalarGridSpec(
            num_scalar_prefetch=1,
            grid=(count,),
            in_specs=[full(a.shape) for a in acts]
            + [
                pl.BlockSpec((g.shape[0], width), lambda j, spot: (0, (j + first) ^ spot[0]))
                for g in grads
            ],
            out_specs=pl.BlockSpec((1, depth, width), lambda j, spot: (j, 0, 0)),
            scratch_shapes=[pltpu.VMEM((depth, tokens), BF16)],
        ),
        out_shape=jax.ShapeDtypeStruct((count, depth, width), BF16),
        compiler_params=pltpu.CompilerParams(dimension_semantics=("arbitrary",)),
        cost_estimate=cost(
            2 * tokens * depth * width * count,
            2 * (count * depth * width + tokens * (depth + count * width)),
        ),
        name="weight_grad",
    )(spot, *acts, *grads)


def spread_kernel(half, spot, low, high, low_far, high_far, out):
    block = pl.program_id(1) ^ spot[0]
    mine = pl.program_id(0) == spot[1]
    for own, near, source in (
        (True, True, low),
        (True, False, high),
        (False, True, low_far),
        (False, False, high_far),
    ):

        @pl.when((mine == own) & ((block < half) == near))
        def _(source=source):
            out[...] = source[0].astype(F32)


def spread_call(low, high, low_far, high_far, spot):
    half, depth, width = low.shape

    def spec(own, near):
        def index(h, i, spot):
            block = i ^ spot[0]
            used = ((h == spot[1]) == own) & ((block < half) == near)
            return (jnp.where(used, block & (half - 1), 0), 0, 0)

        return pl.BlockSpec((1, depth, width), index)

    return pl.pallas_call(
        functools.partial(spread_kernel, half),
        grid_spec=pltpu.PrefetchScalarGridSpec(
            num_scalar_prefetch=1,
            grid=(2, 2 * half),
            in_specs=[spec(True, True), spec(True, False), spec(False, True), spec(False, False)],
            out_specs=pl.BlockSpec((depth, width), lambda h, i, spot: (h, i)),
        ),
        out_shape=jax.ShapeDtypeStruct((2 * depth, 2 * half * width), F32),
        compiler_params=pltpu.CompilerParams(dimension_semantics=("arbitrary", "arbitrary")),
        cost_estimate=cost(0, 4 * half * depth * width * 6),
        name="spread",
    )(spot, low, high, low_far, high_far)


def sum_of(terms, begin, end):
    total = terms[0][begin:end].astype(F32)
    for term in terms[1:]:
        total = total + term[begin:end].astype(F32)
    return total.astype(BF16)


def pick(values, index, width):
    return lax.dynamic_slice_in_dim(values, index * width, width, 1)


def weight_grad(act, grad):
    groups, me = lax.axis_size("fsdp"), lax.axis_index("fsdp")
    core = lax.axis_index("rep") & 1
    half = act.shape[1] // groups // 2
    if groups == 2:
        acts = [pick(act, me, 2 * half), swap(pick(act, 1 - me, 2 * half), "fsdp", 1)]
        grads = [grad, swap(grad, "fsdp", 1)]
    else:
        acts = [lax.all_to_all(act, "fsdp", split_axis=1, concat_axis=0, tiled=True)]
        grads = [lax.all_gather(grad, "fsdp", axis=0, tiled=True)]
    acts = [pick(a, core, half) for a in acts] + [
        swap(pick(a, 1 - core, half), "rep", 1) for a in acts
    ]
    grads = grads + [swap(g, "rep", 1) for g in grads]

    bits = [("rep", m) for m in reversed(masks("rep")) if m > 1] + [("seq", m) for m in masks("seq")]
    count = 2 ** len(bits)
    place = jnp.int32(0)
    for axis, mask in bits:
        place = 2 * place + jnp.where(lax.axis_index(axis) & mask, 1, 0)
    spot = place.reshape(1).astype(jnp.int32)
    send = grad_call(acts, grads, spot, count // 2, count // 2, count)
    keep = grad_call(acts, grads, spot, count // 2, 0, count)
    terms, size = [keep], count // 2
    for level, (axis, mask) in enumerate(bits):
        terms.append(swap(send, axis, mask))
        if level + 1 < len(bits):
            send = sum_of(terms, size // 2, size)
            size //= 2
    low = sum_of(terms, 0, 1)
    for axis, mask in reversed(bits[1:]):
        low = jnp.concatenate([low, swap(low, axis, mask)], axis=0)
    high = swap(low, *bits[0])
    low_far, high_far = swap(low, "rep", 1), swap(high, "rep", 1)
    where = jnp.stack([place, core]).astype(jnp.int32)
    return spread_call(low, high, low_far, high_far, where)


def local(
    tokens,
    conditioning,
    cotangent,
    ada_weight,
    ada_bias,
    qkv_weight,
    qv_bias,
    proj_weight,
    proj_bias,
    fc1_weight,
    fc1_bias,
    fc2_weight,
    fc2_bias,
):
    groups, me = lax.axis_size("fsdp"), lax.axis_index("fsdp")
    parts, at = lax.axis_size("seq"), lax.axis_index("seq")
    local_tokens = tokens[0]
    n_tok, model_width = local_tokens.shape
    share = ada_weight.shape[0]
    fsdp_steps = [("fsdp", m) for m in masks("fsdp")]
    rep_steps = [("rep", m) for m in masks("rep")]

    qkv_blocks = whole_weight(qkv_weight, ("rep", 2))
    proj_blocks = whole_weight(proj_weight, ("seq", 1))
    fc1_blocks = whole_weight(fc1_weight, ("rep", 2))
    fc2_blocks = whole_weight(fc2_weight, ("seq", 1))

    cond_f = conditioning.astype(F32)
    silu_cond = jax.nn.silu(cond_f).astype(BF16)
    biases = (ada_bias, qv_bias, proj_bias, fc1_bias, fc2_bias)
    packed = jnp.concatenate([silu_cond] + [b[None, :] for b in biases], axis=1)
    rows = gather_rows(packed, fsdp_steps)
    silu_rows = rows[:, : silu_cond.shape[1]]
    own_cols = lax.dynamic_slice_in_dim(silu_rows, me * share, share, 1)
    partial = product(own_cols, ada_weight)
    mods = partial[0]
    for j in range(1, groups):
        mods = mods + swap(partial[j], "fsdp", j)
    ordered, at_col, whole_bias = natural(rows, "fsdp"), silu_cond.shape[1], []
    for b in biases:
        whole_bias.append(ordered[:, at_col : at_col + b.shape[0]].reshape(-1).astype(F32))
        at_col += b.shape[0]
    adab, qvb, projb, fc1b, fc2b = whole_bias
    mods = mods + adab
    shift_attn, scale_attn, gate_attn, shift_mlp, scale_mlp, gate_mlp = jnp.split(mods, 6)
    silu_all = gather_rows(own_cols, rep_steps)

    tokens_f = local_tokens.astype(F32)
    normed1, inv_std1 = layer_norm(tokens_f)
    hidden1 = (normed1 * (1.0 + scale_attn) + shift_attn).astype(BF16)
    group = model_width // parts
    qkv_bias = jnp.concatenate([qvb[:model_width], jnp.zeros_like(qvb[:model_width]), qvb[model_width:]])

    def finish_qkv(acc, extras, outs):
        outs[0][0] = (acc + extras[0][...]).astype(BF16)

    (qkv_groups,) = columns_call(
        "qkv",
        hidden1,
        full(hidden1.shape),
        qkv_blocks,
        group,
        False,
        finish_qkv,
        [qkv_bias[None, :]],
        [pl.BlockSpec((1, group), lambda i, o: (0, i))],
        [jax.ShapeDtypeStruct((parts, n_tok, 3 * group), BF16)],
        [pl.BlockSpec((1, n_tok, group), lambda i, o: (i % parts, 0, i // parts))],
    )

    def spread_groups(stack):
        got = []
        for j in range(parts):
            block = lax.dynamic_index_in_dim(stack, at ^ j, 0, keepdims=False)
            got.append(block if j == 0 else swap(block, "seq", j))
        return got

    def return_groups(stack):
        return [stack[0]] + [swap(stack[j], "seq", j) for j in range(1, parts)]

    qkv_heads = spread_groups(qkv_groups)
    attended = heads_call(return_groups(attend_call(qkv_heads)), 1)

    def finish_plain(acc, extras, outs):
        outs[0][...] = acc + extras[0][...]

    wide = min(512, model_width)
    (branch,) = columns_call(
        "proj",
        attended,
        full(attended.shape),
        proj_blocks,
        wide,
        False,
        finish_plain,
        [projb[None, :]],
        [pl.BlockSpec((1, wide), lambda i, o: (0, i))],
        [jax.ShapeDtypeStruct((n_tok, model_width), F32)],
        [pl.BlockSpec((n_tok, wide), lambda i, o: (0, i))],
    )
    middle = tokens_f + gate_attn * branch
    normed2, inv_std2 = layer_norm(middle)
    hidden2 = (normed2 * (1.0 + scale_mlp) + shift_mlp).astype(BF16)

    def finish_gelu(acc, extras, outs):
        gelu_val, gelu_slope = gelu_parts(acc + extras[0][...])
        outs[0][...] = gelu_val.astype(BF16)
        outs[1][...] = gelu_slope

    hidden = fc1_weight.shape[1]
    active, slope = columns_call(
        "fc1",
        hidden2,
        full(hidden2.shape),
        fc1_blocks,
        wide,
        False,
        finish_gelu,
        [fc1b[None, :]],
        [pl.BlockSpec((1, wide), lambda i, o: (0, i))],
        [jax.ShapeDtypeStruct((n_tok, hidden), BF16), jax.ShapeDtypeStruct((n_tok, hidden), F32)],
        [pl.BlockSpec((n_tok, wide), lambda i, o: (0, i))] * 2,
    )
    cot_f = cotangent[0].astype(F32)
    mlp_grad = (gate_mlp * cot_f).astype(BF16)
    fc2_sum = weight_grad(active, mlp_grad)
    mlp_out, pre_grad = mlp_call(active, slope, mlp_grad, fc2b[None, :], fc2_blocks)
    output = (middle + gate_mlp * mlp_out).astype(BF16)
    gate_mlp_grad = jnp.sum(cot_f * mlp_out, axis=0)

    fc1_sum = weight_grad(hidden2, pre_grad)

    def finish_back(acc, extras, outs):
        outs[0][...] = acc

    def back(name, grad, blocks):
        (result,) = columns_call(
            name,
            grad,
            pl.BlockSpec((n_tok, wide), lambda i, o: (0, i)),
            blocks,
            wide,
            True,
            finish_back,
            [],
            [],
            [jax.ShapeDtypeStruct((n_tok, model_width), F32)],
            [full((n_tok, model_width))],
        )
        return result

    hidden2_grad = back("fc1_back", pre_grad, fc1_blocks)
    shift_mlp_grad = jnp.sum(hidden2_grad, axis=0)
    scale_mlp_grad = jnp.sum(hidden2_grad * normed2, axis=0)
    middle_grad = cot_f + norm_back(normed2, inv_std2, hidden2_grad * (1.0 + scale_mlp))
    gate_attn_grad = jnp.sum(middle_grad * branch, axis=0)
    branch_grad = (gate_attn * middle_grad).astype(BF16)

    def finish_groups(acc, extras, outs):
        for g in range(parts):
            outs[0][g] = acc[:, g * group : (g + 1) * group].astype(BF16)

    (attended_grad,) = columns_call(
        "proj_back",
        branch_grad,
        pl.BlockSpec((n_tok, wide), lambda i, o: (0, i)),
        proj_blocks,
        wide,
        True,
        finish_groups,
        [],
        [],
        [jax.ShapeDtypeStruct((parts, n_tok, group), BF16)],
        [full((parts, n_tok, group))],
    )
    proj_sum = weight_grad(attended, branch_grad)
    grad_heads = spread_groups(attended_grad)
    qkv_grad = heads_call(return_groups(attend_back_call(qkv_heads, grad_heads)), 3)
    qkv_sum = weight_grad(hidden1, qkv_grad)
    hidden1_grad = back("qkv_back", qkv_grad, qkv_blocks)
    shift_attn_grad = jnp.sum(hidden1_grad, axis=0)
    scale_attn_grad = jnp.sum(hidden1_grad * normed1, axis=0)
    tokens_grad = middle_grad + norm_back(normed1, inv_std1, hidden1_grad * (1.0 + scale_attn))

    def latent_rows(values):
        row = jnp.concatenate(values)[None, :]
        for mask in masks("seq"):
            row = row + swap(row, "seq", mask)
        return gather_rows(row, fsdp_steps + rep_steps)

    def column_sum(values):
        return jnp.sum(values.astype(F32), axis=0)

    early = latent_rows(
        [gate_attn_grad, shift_mlp_grad, scale_mlp_grad, gate_mlp_grad]
        + [column_sum(branch_grad), column_sum(pre_grad), column_sum(mlp_grad)]
    )
    late = latent_rows(
        [shift_attn_grad, scale_attn_grad]
        + [column_sum(qkv_grad[:, :model_width]), column_sum(qkv_grad[:, 2 * model_width :])]
    )
    two, four = 2 * model_width, 4 * model_width
    mods_rows = jnp.concatenate([late[:, :two], early[:, :four]], axis=1)
    bias_sums = jnp.sum(jnp.concatenate([late[:, two:], early[:, four:]], axis=1), axis=0)

    def own(values):
        length = values.shape[0] // groups
        return lax.dynamic_slice_in_dim(values, me * length, length, 0)

    ends = [0, two, two + model_width, two + model_width + hidden, 2 * two + hidden]
    qv_sum, projb_sum, fc1b_sum, fc2b_sum = (
        own(bias_sums[begin:end]) for begin, end in zip(ends[:-1], ends[1:])
    )
    adab_sum = own(jnp.sum(mods_rows, axis=0))
    ada_sum = lax.dot_general(
        silu_all.astype(F32),
        mods_rows,
        (((0,), (0,)), ((), ())),
        precision=lax.Precision.HIGHEST,
    )
    cond_part = lax.dot_general(
        mods_rows[:groups],
        ada_weight.astype(F32),
        (((1,), (1,)), ((), ())),
        precision=lax.Precision.HIGHEST,
    )
    pieces = [cond_part[:1]] + [swap(cond_part[j : j + 1], "fsdp", j) for j in range(1, groups)]
    cond_sum = natural(jnp.concatenate(pieces, axis=0), "fsdp").reshape(1, -1)
    cond_grad = cond_sum * silu_slope(cond_f)
    return (
        output[None],
        tokens_grad[None],
        cond_grad,
        ada_sum,
        adab_sum,
        qkv_sum,
        qv_sum,
        proj_sum,
        projb_sum,
        fc1_sum,
        fc1b_sum,
        fc2_sum,
        fc2b_sum,
    )


def solution(mesh):
    in_specs = (
        P(("rep", "fsdp"), "seq", None),
        P(("rep", "fsdp"), None),
        P(("rep", "fsdp"), "seq", None),
        P("fsdp", None),
        P("fsdp"),
        P("fsdp", None),
        P("fsdp"),
        P("fsdp", None),
        P("fsdp"),
        P("fsdp", None),
        P("fsdp"),
        P("fsdp", None),
        P("fsdp"),
    )
    out_specs = (
        P(("rep", "fsdp"), "seq", None),
        P(("rep", "fsdp"), "seq", None),
        P(("rep", "fsdp"), None),
        P("fsdp", None),
        P("fsdp"),
        P("fsdp", None),
        P("fsdp"),
        P("fsdp", None),
        P("fsdp"),
        P("fsdp", None),
        P("fsdp"),
        P("fsdp", None),
        P("fsdp"),
    )
    return jax.shard_map(local, mesh=mesh, in_specs=in_specs, out_specs=out_specs, check_vma=False)
```

```python
import functools

import jax
import jax.numpy as jnp
from jax import lax
from jax.experimental import pallas as pl
from jax.experimental.pallas import tpu as pltpu
from jax.sharding import PartitionSpec as P

HEADS = 16
HEAD_DIM = 64


EPSILON = 1e-06
TANH_ROOT = 0.7978845608028654
CUBIC_COEF = 0.044715

F32 = jnp.float32
BF16 = jnp.bfloat16


def product(left_op, right_op):
    return jnp.dot(left_op, right_op, preferred_element_type=F32)


def product_tn(left_op, right_op):
    return lax.dot_general(
        left_op, right_op, (((0,), (0,)), ((), ())), preferred_element_type=F32
    )


def product_nt(left_op, right_op):
    return lax.dot_general(
        left_op, right_op, (((1,), (1,)), ((), ())), preferred_element_type=F32
    )


def gelu_parts(pre_act):
    tanh_val = jnp.tanh(TANH_ROOT * (pre_act + CUBIC_COEF * pre_act * pre_act * pre_act))
    gelu_val = 0.5 * pre_act * (1.0 + tanh_val)
    gelu_slope = 0.5 * (1.0 + tanh_val) + 0.5 * pre_act * (
        1.0 - tanh_val * tanh_val
    ) * TANH_ROOT * (1.0 + 3.0 * CUBIC_COEF * pre_act * pre_act)
    return (gelu_val, gelu_slope)


def layer_norm(values):
    center = values - jnp.mean(values, axis=-1, keepdims=True)
    inv_std = lax.rsqrt(jnp.mean(center * center, axis=-1, keepdims=True) + EPSILON)
    return (center * inv_std, inv_std)


def norm_back(normed, inv_std, grad_in):
    return inv_std * (
        grad_in
        - jnp.mean(grad_in, axis=-1, keepdims=True)
        - normed * jnp.mean(grad_in * normed, axis=-1, keepdims=True)
    )


def silu_slope(condition):
    sigmoid_c = jax.nn.sigmoid(condition)
    return sigmoid_c * (1.0 + condition * (1.0 - sigmoid_c))


def swap(value, axis, mask):
    size = lax.axis_size(axis)
    return lax.ppermute(value, axis, [(i, i ^ mask) for i in range(size)])


def masks(axis):
    size, found, mask = lax.axis_size(axis), [], 1
    while mask < size:
        found.append(mask)
        mask *= 2
    return found


def gather_rows(value, steps):
    for axis, mask in steps:
        value = jnp.concatenate([value, swap(value, axis, mask)], axis=0)
    return value


def natural(stack, axis):
    me = lax.axis_index(axis)
    return jnp.concatenate(
        [lax.dynamic_slice_in_dim(stack, me ^ i, 1, 0) for i in range(stack.shape[0])], axis=0
    )


def after(value, *deps):
    return lax.optimization_barrier((value, deps))[0]


class Order:
    def __init__(self):
        self.token = ()

    def gate(self, value):
        return after(value, self.token)

    def done(self, *token):
        self.token = token


class Weight:
    def __init__(self, weight, relay):
        self.weight, self.relay_step = weight, relay
        self.paired = lax.axis_size("fsdp") == 2
        self.rows = weight.shape[0]
        self.piece = self.rows // 4
        axis, mask = relay
        far = jnp.where(lax.axis_index(axis) & mask, 2, 0)
        self.here = far + (lax.axis_index("rep") & 1)
        if self.paired:
            self.first = lax.dynamic_slice_in_dim(weight, self.here * self.piece, self.piece, 0)

    def fetch(self, order=None):
        if self.paired:
            quarter = self.first if order is None else order.gate(self.first)
            self.first = swap(quarter, "fsdp", 1)
        else:
            self.first = self.weight if order is None else order.gate(self.weight)
            self.first = lax.all_gather(self.first, "fsdp", axis=0, tiled=True)

    def relay(self, order=None):
        if self.paired:
            if order is not None:
                self.first = order.gate(self.first)
            self.second = swap(self.first, *self.relay_step)
            self.third = swap(self.first, "rep", 1)

    def cross(self, order=None):
        if self.paired:
            if order is not None:
                self.second = order.gate(self.second)
            self.fourth = swap(self.second, "rep", 1)

    def blocks(self):
        if not self.paired:
            return [(jnp.int32(0), self.first)]
        me = lax.axis_index("fsdp")
        peer, here, piece = (1 - me) * self.rows, self.here, self.piece
        return [
            (me * self.rows, self.weight),
            (peer + here * piece, self.first),
            (peer + (here ^ 1) * piece, self.third),
            (peer + (here ^ 2) * piece, self.second),
            (peer + (here ^ 3) * piece, self.fourth),
        ]


ANY = pl.BlockSpec(memory_space=pl.ANY)


def full(shape):
    return pl.BlockSpec(shape, lambda *_: (0,) * len(shape))


def cost(flops, nbytes, trans=0):
    return pl.CostEstimate(flops=int(flops), bytes_accessed=int(nbytes), transcendentals=int(trans))


def columns_kernel(sizes, tile, tiles, back, finish, n_extra, n_out, offs, act, *refs):
    n = len(sizes)
    weights, extras, outs = refs[:n], refs[n : n + n_extra], refs[n + n_extra : n + n_extra + n_out]
    buf, sems = refs[n + n_extra + n_out :]

    def copies(at):
        cols = pl.ds(at * tile, tile)
        return [
            pltpu.make_async_copy(
                w.at[:, cols],
                buf.at[at, pl.ds(pl.multiple_of(offs[b], 16), sizes[b]), :],
                sems.at[at, b],
            )
            for b, w in enumerate(weights)
        ]

    for at in range(tiles):
        for c in copies(at):
            c.start()
    total = None
    for at in range(tiles):
        for c in copies(at):
            c.wait()
        if back:
            part = product_nt(act[:, at * tile : (at + 1) * tile], buf[at])
            total = part if total is None else total + part
        else:
            finish(at, product(act[...], buf[at]), extras, outs)
    if back:
        finish(0, total, extras, outs)


def columns_call(name, act, blocks, tile, back, finish, extras, outs):
    offs = jnp.stack([o for o, _ in blocks]).astype(jnp.int32)
    weights = [w for _, w in blocks]
    sizes = [w.shape[0] for w in weights]
    depth, width = sum(sizes), weights[0].shape[1]
    n_tok, tiles = act.shape[0], width // tile
    vm = pl.BlockSpec(memory_space=pltpu.VMEM)
    return pl.pallas_call(
        functools.partial(columns_kernel, sizes, tile, tiles, back, finish, len(extras), len(outs)),
        in_specs=[pl.BlockSpec(memory_space=pltpu.SMEM), vm]
        + [ANY] * len(weights)
        + [vm] * len(extras),
        out_specs=[vm] * len(outs),
        out_shape=list(outs),
        scratch_shapes=[
            pltpu.VMEM((tiles, depth, tile), BF16),
            pltpu.SemaphoreType.DMA((tiles, len(sizes))),
        ],
        cost_estimate=cost(2 * n_tok * depth * width, 2 * depth * width),
        name=name,
    )(offs, act, *weights, *extras)


def mlp_kernel(plan, tile, offs, active, slope, mlp_grad, bias, *refs):
    n = 1 + max(b for b, _ in plan)
    weights = refs[:n]
    out, pre_grad, buf, sems = refs[n:]

    def copy(s):
        b, at = plan[s]
        return pltpu.make_async_copy(
            weights[b].at[pl.ds(at, tile), :], buf.at[s], sems.at[s]
        )

    for s in range(len(plan)):
        copy(s).start()
    out[...] = jnp.broadcast_to(bias[...], out.shape)
    for s in range(len(plan)):
        copy(s).wait()
        cols = pl.ds(pl.multiple_of(offs[s], 128), tile)
        out[...] += product(active[:, cols], buf[s])
        pre_grad[:, cols] = (product_nt(mlp_grad[...], buf[s]) * slope[:, cols]).astype(BF16)


def mlp_call(active, slope, mlp_grad, bias, blocks):
    n_tok, hidden = active.shape
    width = mlp_grad.shape[1]
    tile = min([w.shape[0] for _, w in blocks] + [512])
    plan, offs = [], []
    for b, (o, w) in enumerate(blocks):
        for at in range(0, w.shape[0], tile):
            plan.append((b, at))
            offs.append(o + at)
    vm = pl.BlockSpec(memory_space=pltpu.VMEM)
    return pl.pallas_call(
        functools.partial(mlp_kernel, plan, tile),
        in_specs=[pl.BlockSpec(memory_space=pltpu.SMEM)] + [vm] * 4 + [ANY] * len(blocks),
        out_specs=[vm, vm],
        out_shape=[
            jax.ShapeDtypeStruct((n_tok, width), F32),
            jax.ShapeDtypeStruct((n_tok, hidden), BF16),
        ],
        scratch_shapes=[
            pltpu.VMEM((len(plan), tile, width), BF16),
            pltpu.SemaphoreType.DMA((len(plan),)),
        ],
        cost_estimate=cost(4 * n_tok * hidden * width, 2 * hidden * width),
        name="mlp_both",
    )(jnp.stack(offs).astype(jnp.int32), active, slope, mlp_grad, bias, *[w for _, w in blocks])


def softmax_of(query, key):
    scores = product_nt(query, key) * (HEAD_DIM**-0.5)
    exponent = jnp.exp(scores - jnp.max(scores, axis=-1, keepdims=True))
    return exponent * (1.0 / jnp.sum(exponent, axis=-1, keepdims=True))


def attend_kernel(n, width, *refs):
    blocks, out = refs[:n], refs[n]
    n_tok = blocks[0].shape[0]

    def part(at):
        return jnp.concatenate([b[:, at : at + HEAD_DIM] for b in blocks], axis=0)

    for head in range(0, width, HEAD_DIM):
        probs = softmax_of(part(head), part(width + head)).astype(BF16)
        attended = product(probs, part(2 * width + head)).astype(BF16)
        for j in range(n):
            out[j, :, head : head + HEAD_DIM] = attended[j * n_tok : (j + 1) * n_tok]


def attend_call(blocks):
    n, n_tok, width = len(blocks), blocks[0].shape[0], blocks[0].shape[1] // 3
    vm = pl.BlockSpec(memory_space=pltpu.VMEM)
    pairs = (n * n_tok) ** 2
    return pl.pallas_call(
        functools.partial(attend_kernel, n, width),
        in_specs=[vm] * n,
        out_specs=vm,
        out_shape=jax.ShapeDtypeStruct((n, n_tok, width), BF16),
        cost_estimate=cost(4 * pairs * width, 8 * n * n_tok * width, pairs * width // HEAD_DIM),
        name="attend",
    )(*blocks)


def attend_back_kernel(n, width, *refs):
    blocks, grads, out = refs[:n], refs[n : 2 * n], refs[2 * n]
    n_tok = blocks[0].shape[0]

    def part(of, at):
        return jnp.concatenate([b[:, at : at + HEAD_DIM] for b in of], axis=0)

    scale = HEAD_DIM**-0.5
    for head in range(0, width, HEAD_DIM):
        query, key = part(blocks, head), part(blocks, width + head)
        value, grad = part(blocks, 2 * width + head), part(grads, head)
        probs = softmax_of(query, key)
        prob_grad = product_nt(grad, value)
        row_delta = jnp.sum(probs * prob_grad, axis=-1, keepdims=True)
        score_grad = (probs * (prob_grad - row_delta) * scale).astype(BF16)
        parts = (
            product(score_grad, key),
            product_tn(score_grad, query),
            product_tn(probs.astype(BF16), grad),
        )
        for at, value_of in enumerate(parts):
            rounded = value_of.astype(BF16)
            for j in range(n):
                out[j, :, at * width + head : at * width + head + HEAD_DIM] = rounded[
                    j * n_tok : (j + 1) * n_tok
                ]


def attend_back_call(blocks, grads):
    n, n_tok, width = len(blocks), blocks[0].shape[0], blocks[0].shape[1] // 3
    vm = pl.BlockSpec(memory_space=pltpu.VMEM)
    pairs = (n * n_tok) ** 2
    return pl.pallas_call(
        functools.partial(attend_back_kernel, n, width),
        in_specs=[vm] * (2 * n),
        out_specs=vm,
        out_shape=jax.ShapeDtypeStruct((n, n_tok, 3 * width), BF16),
        cost_estimate=cost(10 * pairs * width, 14 * n * n_tok * width, pairs * width // HEAD_DIM),
        name="attend_back",
    )(*blocks, *grads)


def heads_kernel(n, parts, me, *refs):
    blocks, out = refs[:n], refs[n]
    width = blocks[0].shape[1] // parts
    for j in range(n):
        for p in range(parts):
            at = pl.multiple_of(p * n * width + (me[0] ^ j) * width, 128)
            out[:, pl.ds(at, width)] = blocks[j][:, p * width : (p + 1) * width]


def heads_call(blocks, parts):
    n, (n_tok, width) = len(blocks), blocks[0].shape
    vm = pl.BlockSpec(memory_space=pltpu.VMEM)
    return pl.pallas_call(
        functools.partial(heads_kernel, n, parts),
        in_specs=[pl.BlockSpec(memory_space=pltpu.SMEM)] + [vm] * n,
        out_specs=vm,
        out_shape=jax.ShapeDtypeStruct((n_tok, n * width), BF16),
        cost_estimate=cost(0, 4 * n * n_tok * width),
        name="heads",
    )(lax.axis_index("seq").reshape(1).astype(jnp.int32), *blocks)


def grad_kernel(n, count, spot, *refs):
    acts, grads, keep, send = refs[:n], refs[n : 2 * n], refs[2 * n], refs[2 * n + 1]
    flipped = jnp.concatenate([a[...].T for a in acts], axis=1)
    width = keep.shape[2]
    for j in list(range(count // 2, count)) + list(range(count // 2)):
        cols = pl.ds(pl.multiple_of((spot[0] ^ j) * width, 128), width)
        rows = jnp.concatenate([g[:, cols] for g in grads], axis=0)
        block = product(flipped, rows).astype(BF16)
        if j < count // 2:
            keep[j] = block
        else:
            send[j - count // 2] = block


def grad_call(acts, grads, spot, count):
    depth, width = acts[0].shape[1], grads[0].shape[1] // count
    tokens = sum(a.shape[0] for a in acts)
    vm = pl.BlockSpec(memory_space=pltpu.VMEM)
    return pl.pallas_call(
        functools.partial(grad_kernel, len(acts), count),
        in_specs=[pl.BlockSpec(memory_space=pltpu.SMEM)] + [vm] * (2 * len(acts)),
        out_specs=[vm, vm],
        out_shape=[jax.ShapeDtypeStruct((count // 2, depth, width), BF16)] * 2,
        cost_estimate=cost(
            2 * tokens * depth * width * count,
            2 * (count * depth * width + tokens * (depth + count * width)),
        ),
        name="weight_grad",
    )(spot, *acts, *grads)


def spread_kernel(half, spot, low, high, low_far, high_far, out, wide, sems):
    depth, width = low.shape[1:]
    waits = []
    for far, sources in enumerate(((low, high), (low_far, high_far))):
        for j in range(2 * half):
            at = far * 2 * half + j
            wide[at] = sources[j // half][j % half].astype(F32)
            row = pl.multiple_of((spot[1] ^ far) * depth, 8)
            col = pl.multiple_of((spot[0] ^ j) * width, 128)
            copy = pltpu.make_async_copy(
                wide.at[at], out.at[pl.ds(row, depth), pl.ds(col, width)], sems.at[at]
            )
            copy.start()
            waits.append(copy)
    for copy in waits:
        copy.wait()


def spread_call(low, high, low_far, high_far, spot):
    half, depth, width = low.shape
    vm = pl.BlockSpec(memory_space=pltpu.VMEM)
    return pl.pallas_call(
        functools.partial(spread_kernel, half),
        in_specs=[pl.BlockSpec(memory_space=pltpu.SMEM)] + [vm] * 4,
        out_specs=ANY,
        out_shape=jax.ShapeDtypeStruct((2 * depth, 2 * half * width), F32),
        scratch_shapes=[
            pltpu.VMEM((4 * half, depth, width), F32),
            pltpu.SemaphoreType.DMA((4 * half,)),
        ],
        cost_estimate=cost(0, 4 * half * depth * width * 6),
        name="spread",
    )(spot, low, high, low_far, high_far)


def sum_of(terms, begin, end):
    total = terms[0][begin:end].astype(F32)
    for term in terms[1:]:
        total = total + term[begin:end].astype(F32)
    return total.astype(BF16)


def pick(values, index, width):
    return lax.dynamic_slice_in_dim(values, index * width, width, 1)


class WeightGrad:
    def __init__(self, act, grad):
        groups, me = lax.axis_size("fsdp"), lax.axis_index("fsdp")
        self.core = lax.axis_index("rep") & 1
        self.half = act.shape[1] // groups // 2
        self.near, self.far = [], []
        if groups == 2:
            self.near = [pick(act, me, 2 * self.half), grad]
            self.far = [
                swap(pick(act, 1 - me, 2 * self.half), "fsdp", 1),
                swap(grad, "fsdp", 1),
            ]
        else:
            self.far = [
                lax.all_to_all(act, "fsdp", split_axis=1, concat_axis=0, tiled=True),
                lax.all_gather(grad, "fsdp", axis=0, tiled=True),
            ]
        self.bits = [("rep", m) for m in reversed(masks("rep")) if m > 1]
        self.bits += [("seq", m) for m in masks("seq")]
        self.count = 2 ** len(self.bits)
        self.place = jnp.int32(0)
        for axis, mask in self.bits:
            self.place = 2 * self.place + jnp.where(lax.axis_index(axis) & mask, 1, 0)
        self.acts, self.grads = [], []

    def cross(self, pair):
        act, grad = pair
        self.acts += [
            pick(act, self.core, self.half),
            swap(pick(act, 1 - self.core, self.half), "rep", 1),
        ]
        self.grads += [grad, swap(grad, "rep", 1)]

    def cross_near(self, order):
        if self.near:
            self.cross(order.gate(self.near))

    def cross_far(self, order):
        self.cross(order.gate(self.far))

    def multiply(self, order):
        spot = self.place.reshape(1).astype(jnp.int32)
        acts, grads = order.gate((self.acts, self.grads))
        keep, send = grad_call(acts, grads, spot, self.count)
        order.done(keep, send)
        self.terms, self.level = [keep], 0
        self.pending = swap(send, *self.bits[0])

    def reduce(self, order):
        if self.level == len(self.bits):
            return
        self.terms.append(order.gate(self.pending))
        self.level += 1
        size = self.count >> self.level
        if self.level < len(self.bits):
            send = sum_of(self.terms, size // 2, size)
            self.pending = swap(send, *self.bits[self.level])
        else:
            send = sum_of(self.terms, 0, 1)
            self.low = send
            self.back = self.level - 1
            self.pending = swap(send, *self.bits[self.back])
        order.done(send)

    def gather(self, order):
        while self.level < len(self.bits):
            self.reduce(order)
        if self.back < 0:
            return
        got = order.gate(self.pending)
        if self.back:
            self.low = jnp.concatenate([self.low, got], axis=0)
            self.back -= 1
            self.pending = swap(self.low, *self.bits[self.back])
            if not self.back:
                self.low_far = swap(self.low, "rep", 1)
            order.done(self.low)
        else:
            self.high = got
            self.high_far = swap(self.high, "rep", 1)
            self.back -= 1
            order.done(self.high)

    def spread(self, order):
        while self.level < len(self.bits) or self.back >= 0:
            self.gather(order)
        where = jnp.stack([self.place, self.core]).astype(jnp.int32)
        parts = order.gate((self.low, self.high, self.low_far, self.high_far))
        result = spread_call(*parts, where)
        order.done(result)
        return result


def local(
    tokens,
    conditioning,
    cotangent,
    ada_weight,
    ada_bias,
    qkv_weight,
    qv_bias,
    proj_weight,
    proj_bias,
    fc1_weight,
    fc1_bias,
    fc2_weight,
    fc2_bias,
):
    groups, me = lax.axis_size("fsdp"), lax.axis_index("fsdp")
    parts, at = lax.axis_size("seq"), lax.axis_index("seq")
    local_tokens = tokens[0]
    n_tok, model_width = local_tokens.shape
    share = ada_weight.shape[0]
    fsdp_steps = [("fsdp", m) for m in masks("fsdp")]
    rep_steps = [("rep", m) for m in masks("rep")]

    order = Order()
    qkv_w = Weight(qkv_weight, ("rep", 2))
    proj_w = Weight(proj_weight, ("seq", 1))
    fc1_w = Weight(fc1_weight, ("rep", 2))
    fc2_w = Weight(fc2_weight, ("seq", 1))
    qkv_w.fetch()

    cond_f = conditioning.astype(F32)
    silu_cond = jax.nn.silu(cond_f).astype(BF16)
    biases = (ada_bias, qv_bias, proj_bias, fc1_bias, fc2_bias)
    packed = jnp.concatenate([silu_cond] + [b[None, :] for b in biases], axis=1)
    rows = gather_rows(packed, fsdp_steps)
    silu_rows = rows[:, : silu_cond.shape[1]]
    own_cols = lax.dynamic_slice_in_dim(silu_rows, me * share, share, 1)
    partial = product(own_cols, ada_weight)
    mods = partial[0]
    for j in range(1, groups):
        mods = mods + swap(partial[j], "fsdp", j)
    ordered, at_col, whole_bias = natural(rows, "fsdp"), silu_cond.shape[1], []
    for b in biases:
        whole_bias.append(ordered[:, at_col : at_col + b.shape[0]].reshape(-1).astype(F32))
        at_col += b.shape[0]
    adab, qvb, projb, fc1b, fc2b = whole_bias
    mods = mods + adab
    order.done(mods)
    proj_w.fetch(order)
    fc1_w.fetch(order)
    fc2_w.fetch(order)
    shift_attn, scale_attn, gate_attn, shift_mlp, scale_mlp, gate_mlp = jnp.split(mods, 6)

    tokens_f = local_tokens.astype(F32)
    normed1, inv_std1 = layer_norm(tokens_f)
    hidden1 = (normed1 * (1.0 + scale_attn) + shift_attn).astype(BF16)
    group = model_width // parts
    qkv_bias = jnp.concatenate([qvb[:model_width], jnp.zeros_like(qvb[:model_width]), qvb[model_width:]])

    def finish_qkv(i, acc, extras, outs):
        bias = extras[0][:, i * group : (i + 1) * group]
        part, g = i // parts, i % parts
        outs[0][g, :, part * group : (part + 1) * group] = (acc + bias).astype(BF16)

    qkv_w.relay()
    proj_w.relay(order)
    order.done(proj_w.first)
    qkv_w.cross(order)
    (qkv_groups,) = columns_call(
        "qkv",
        hidden1,
        qkv_w.blocks(),
        group,
        False,
        finish_qkv,
        [qkv_bias[None, :]],
        [jax.ShapeDtypeStruct((parts, n_tok, 3 * group), BF16)],
    )
    order.done(qkv_groups)

    def spread_groups(stack):
        got = []
        for j in range(parts):
            block = lax.dynamic_index_in_dim(stack, at ^ j, 0, keepdims=False)
            got.append(block if j == 0 else swap(block, "seq", j))
        return got

    def return_groups(stack):
        return [stack[0]] + [swap(stack[j], "seq", j) for j in range(1, parts)]

    qkv_heads = spread_groups(qkv_groups)
    fc1_w.relay(order)
    proj_w.cross(order)
    order.done(qkv_groups, fc1_w.first)
    qkv_heads = order.gate(qkv_heads)
    attended = attend_call(qkv_heads)
    order.done(attended)
    attended = return_groups(attended)
    fc2_w.relay(order)
    order.done(fc2_w.first)
    attended = heads_call(order.gate(attended), 1)
    order.done(attended)
    fc1_w.cross(order)

    def finish_plain(i, acc, extras, outs):
        cols = slice(i * wide, (i + 1) * wide)
        outs[0][:, cols] = acc + extras[0][:, cols]

    wide = min(512, model_width)
    order.done(attended, fc1_w.second if groups == 2 else attended)
    (branch,) = columns_call(
        "proj",
        order.gate(attended),
        proj_w.blocks(),
        wide,
        False,
        finish_plain,
        [projb[None, :]],
        [jax.ShapeDtypeStruct((n_tok, model_width), F32)],
    )
    order.done(branch)
    middle = tokens_f + gate_attn * branch
    normed2, inv_std2 = layer_norm(middle)
    hidden2 = (normed2 * (1.0 + scale_mlp) + shift_mlp).astype(BF16)

    def finish_gelu(i, acc, extras, outs):
        cols = slice(i * wide, (i + 1) * wide)
        gelu_val, gelu_slope = gelu_parts(acc + extras[0][:, cols])
        outs[0][:, cols] = gelu_val.astype(BF16)
        outs[1][:, cols] = gelu_slope

    hidden = fc1_weight.shape[1]
    active, slope = columns_call(
        "fc1",
        hidden2,
        fc1_w.blocks(),
        wide,
        False,
        finish_gelu,
        [fc1b[None, :]],
        [jax.ShapeDtypeStruct((n_tok, hidden), BF16), jax.ShapeDtypeStruct((n_tok, hidden), F32)],
    )
    cot_f = cotangent[0].astype(F32)
    mlp_grad = (gate_mlp * cot_f).astype(BF16)
    fc2_wg = WeightGrad(active, order.gate(mlp_grad))
    order.done(active)
    fc2_w.cross(order)
    mlp_out, pre_grad = mlp_call(active, slope, mlp_grad, fc2b[None, :], fc2_w.blocks())
    order.done(pre_grad)
    fc2_wg.cross_near(order)
    output = (middle + gate_mlp * mlp_out).astype(BF16)
    gate_mlp_grad = jnp.sum(cot_f * mlp_out, axis=0)

    fc1_wg = WeightGrad(hidden2, pre_grad)

    def finish_back(i, acc, extras, outs):
        outs[0][...] = acc

    def back(name, grad, blocks):
        (result,) = columns_call(
            name,
            grad,
            blocks,
            wide,
            True,
            finish_back,
            [],
            [jax.ShapeDtypeStruct((n_tok, model_width), F32)],
        )
        return result

    hidden2_grad = back("fc1_back", pre_grad, fc1_w.blocks())
    order.done(hidden2_grad)
    fc2_wg.cross_far(order)
    shift_mlp_grad = jnp.sum(hidden2_grad, axis=0)
    scale_mlp_grad = jnp.sum(hidden2_grad * normed2, axis=0)
    middle_grad = cot_f + norm_back(normed2, inv_std2, hidden2_grad * (1.0 + scale_mlp))
    gate_attn_grad = jnp.sum(middle_grad * branch, axis=0)
    branch_grad = (gate_attn * middle_grad).astype(BF16)
    order.done(branch_grad, *fc2_wg.far)
    proj_wg = WeightGrad(attended, branch_grad)
    fc2_wg.multiply(order)

    def finish_groups(i, acc, extras, outs):
        for g in range(parts):
            outs[0][g] = acc[:, g * group : (g + 1) * group].astype(BF16)

    (attended_grad,) = columns_call(
        "proj_back",
        order.gate(branch_grad),
        proj_w.blocks(),
        wide,
        True,
        finish_groups,
        [],
        [jax.ShapeDtypeStruct((parts, n_tok, group), BF16)],
    )
    order.done(attended_grad)
    grad_heads = spread_groups(attended_grad)
    fc1_wg.cross_near(order)
    fc1_wg.cross_far(order)
    order.done(attended_grad, *fc1_wg.acts, *fc1_wg.grads[::2])
    returned = attend_back_call(qkv_heads, order.gate(grad_heads))
    order.done(returned)
    returned = return_groups(returned)
    fc1_wg.multiply(order)
    fc2_wg.reduce(order)
    proj_wg.cross_near(order)
    proj_wg.cross_far(order)
    proj_wg.multiply(order)
    qkv_grad = heads_call(order.gate(returned), 3)
    order.done(qkv_grad)
    qkv_wg = WeightGrad(hidden1, qkv_grad)
    qkv_wg.cross_near(order)
    hidden1_grad = back("qkv_back", qkv_grad, qkv_w.blocks())
    shift_attn_grad = jnp.sum(hidden1_grad, axis=0)
    scale_attn_grad = jnp.sum(hidden1_grad * normed1, axis=0)
    tokens_grad = middle_grad + norm_back(normed1, inv_std1, hidden1_grad * (1.0 + scale_attn))
    order.done(hidden1_grad)

    def column_sum(values):
        return jnp.sum(values.astype(F32), axis=0)

    small = jnp.concatenate(
        [shift_attn_grad, scale_attn_grad, gate_attn_grad]
        + [shift_mlp_grad, scale_mlp_grad, gate_mlp_grad]
        + [column_sum(qkv_grad[:, :model_width]), column_sum(qkv_grad[:, 2 * model_width :])]
        + [column_sum(branch_grad), column_sum(pre_grad), column_sum(mlp_grad)]
    )[None, :]
    small_steps = [("seq", m) for m in masks("seq")] + rep_steps + fsdp_steps

    def small_step(row):
        axis, mask = small_steps.pop(0)
        got = swap(row, axis, mask)
        order.done(row)
        return (axis, row, got)

    def small_done(state):
        axis, row, got = state
        got = order.gate(got)
        row = row + got if axis == "seq" else jnp.concatenate([row, got], axis=0)
        order.done(row)
        return row

    state = small_step(small)
    fc2_wg.reduce(order)
    fc1_wg.reduce(order)
    state = small_step(small_done(state))
    fc2_wg.reduce(order)
    qkv_wg.cross_far(order)
    qkv_wg.multiply(order)
    proj_wg.reduce(order)
    state = small_step(small_done(state))
    fc1_wg.reduce(order)
    state = small_step(small_done(state))
    fc2_wg.gather(order)
    proj_wg.reduce(order)
    fc1_wg.reduce(order)
    qkv_wg.reduce(order)
    state = small_step(small_done(state))
    fc2_wg.gather(order)
    proj_wg.reduce(order)
    qkv_wg.reduce(order)
    while small_steps:
        state = small_step(small_done(state))
    small_rows = small_done(state)
    fc1_wg.gather(order)
    proj_wg.gather(order)
    qkv_wg.reduce(order)

    silu_all = gather_rows(own_cols, rep_steps)
    small_rows = small_rows.reshape(groups, -1, small_rows.shape[1])
    width = 6 * model_width
    mods_rows, bias_sums = small_rows[..., :width], jnp.sum(small_rows[..., width:], axis=(0, 1))
    cond_rows = mods_rows[:, 0]
    mods_rows = jnp.swapaxes(mods_rows, 0, 1).reshape(-1, width)

    def own(values):
        length = values.shape[0] // groups
        return lax.dynamic_slice_in_dim(values, me * length, length, 0)

    two = 2 * model_width
    ends = [0, two, two + model_width, two + model_width + hidden, 2 * two + hidden]
    qv_sum, projb_sum, fc1b_sum, fc2b_sum = (
        own(bias_sums[begin:end]) for begin, end in zip(ends[:-1], ends[1:])
    )
    adab_sum = own(jnp.sum(mods_rows, axis=0))
    ada_sum = lax.dot_general(
        silu_all.astype(F32),
        mods_rows,
        (((0,), (0,)), ((), ())),
        precision=lax.Precision.HIGHEST,
    )
    cond_part = lax.dot_general(
        cond_rows,
        ada_weight.astype(F32),
        (((1,), (1,)), ((), ())),
        precision=lax.Precision.HIGHEST,
    )
    pieces = [cond_part[:1]] + [swap(cond_part[j : j + 1], "fsdp", j) for j in range(1, groups)]
    fc1_wg.gather(order)
    proj_wg.gather(order)
    qkv_wg.gather(order)
    order.done(order.token, ada_sum)
    fc2_wg.gather(order)
    qkv_wg.gather(order)
    fc2_sum = fc2_wg.spread(order)
    fc1_sum = fc1_wg.spread(order)
    proj_sum = proj_wg.spread(order)
    cond_sum = natural(order.gate(jnp.concatenate(pieces, axis=0)), "fsdp").reshape(1, -1)
    cond_grad = cond_sum * silu_slope(cond_f)
    qkv_sum = qkv_wg.spread(order)
    return (
        output[None],
        tokens_grad[None],
        cond_grad,
        ada_sum,
        adab_sum,
        qkv_sum,
        qv_sum,
        proj_sum,
        projb_sum,
        fc1_sum,
        fc1b_sum,
        fc2_sum,
        fc2b_sum,
    )


def solution(mesh):
    in_specs = (
        P(("rep", "fsdp"), "seq", None),
        P(("rep", "fsdp"), None),
        P(("rep", "fsdp"), "seq", None),
        P("fsdp", None),
        P("fsdp"),
        P("fsdp", None),
        P("fsdp"),
        P("fsdp", None),
        P("fsdp"),
        P("fsdp", None),
        P("fsdp"),
        P("fsdp", None),
        P("fsdp"),
    )
    out_specs = (
        P(("rep", "fsdp"), "seq", None),
        P(("rep", "fsdp"), "seq", None),
        P(("rep", "fsdp"), None),
        P("fsdp", None),
        P("fsdp"),
        P("fsdp", None),
        P("fsdp"),
        P("fsdp", None),
        P("fsdp"),
        P("fsdp", None),
        P("fsdp"),
        P("fsdp", None),
        P("fsdp"),
    )
    return jax.shard_map(local, mesh=mesh, in_specs=in_specs, out_specs=out_specs, check_vma=False)
```
